32 devices in a mesh: freq: 16 (over z, y, core), rows: 2 (over x).
Axes of the slice: x: 2, y: 2, z: 4, core: 2. Of those that a mesh axis runs over, the one named last changes fastest.
Arguments:
- kernel: bfloat16 [2, 128, 2048, 2048], P(None, 'freq', 'rows'), may hold values from -0.25 to 0.25
- tile_mask: int32 [128, 16, 16], P('freq', 'rows'), may hold values 0 or 1
- direct: float32 [2048, 128, 512], P(('rows', 'freq')), may hold values from -6 to 6
- onsets: int32 [2048, 128], P(('rows', 'freq')), may hold values from 64 to 447
Outputs:
- focusing: float32 [2048, 128, 512], P(('rows', 'freq'))
The draws below stay inside these ranges and needn't reach their ends.
Inputs may be any that keep to these rules, and one draw needn't show every extreme that they name: `tile_mask`: 0 drops a tile, 1 keeps it.
All inputs are finite; a program needn't handle non-finite values. No bound on the sum of `tile_mask` on one device may be relied on, other than what follows from the above.
Results may differ from the reference program's by a relative error of at most 0.0026.
Values may be sent and summed in bfloat16 or wider, within the bound.
No kernel may reach another device: no remote copies, remote signals or barrier semaphores. Data moves between devices by JAX's collectives and lax.ppermute only.
A program may use at most 320 MiB of HBM per device.

```python
import math
import jax
import jax.numpy as jnp
from jax import lax

N = 2048
NF = 128
NT = 512
TILE = 128
FOCAL = 128
ITERS = 2


def touch_ends(drawn, stream_key, smallest, largest):
    longest = drawn.shape.index(max(drawn.shape))
    spots = []
    for shift in (0, 1):
        where = [jax.random.randint(jax.random.fold_in(stream_key, axis), (), 0, length) for axis, length in enumerate(drawn.shape)]
        where[longest] = (where[longest] + shift) % drawn.shape[longest]
        spots.append(tuple(where))
    return drawn.at[spots[0]].set(smallest).at[spots[1]].set(largest)


def level_of(stream_key, dims, shards, least, largest):
    def one(position, shards_of):
        heights = jax.random.uniform(jax.random.fold_in(jax.random.fold_in(stream_key, 6), position), (shards_of,), jnp.float32, least / len(shards), largest / len(shards))
        return jnp.repeat(jnp.exp(heights), dims[position] // shards_of).reshape((-1,) + (1,) * (len(dims) - position - 1))

    gain = one(*shards[0])
    for cut in shards[1:]:
        gain = gain * one(*cut)
    return gain


def normal_values(stream_key, extent, scale, bound, split=(), held_as=jnp.bfloat16):
    values = scale * jax.random.normal(stream_key, extent, jnp.float32)
    if split:
        values = values * level_of(stream_key, extent, split, -0.22, 0.18)
    return jnp.clip(values, -bound, bound).astype(held_as)


def setup_inputs(seed: int = 0) -> dict:
    seeds = jax.random.split(jax.random.key(seed), 5)
    kernel = normal_values(seeds[0], (2, NF, N, N), (N // 4) ** -0.5, 0.25, ((1, 16), (2, 2)))
    tile_mask = touch_ends((jax.random.randint(seeds[1], (NF, N // TILE, N // TILE), 0, 8) < 1).astype(jnp.int32), jax.random.fold_in(seeds[1], 1), 0, 1)
    direct = normal_values(seeds[2], (N, FOCAL, NT), 1.0, 6.0, ((0, 32),), jnp.float32)
    onsets = touch_ends(jax.random.randint(seeds[3], (N, FOCAL), NT // 8, 7 * NT // 8), jax.random.fold_in(seeds[3], 1), NT // 8, (7 * NT // 8) - 1).astype(jnp.int32)
    return dict(kernel=kernel, tile_mask=tile_mask, direct=direct, onsets=onsets)


def phase_table():
    freq_ids = jnp.arange(NF, dtype=jnp.int32) + 1
    time_ids = jnp.arange(NT, dtype=jnp.int32)
    phase_ids = freq_ids[:, None] * time_ids[None, :] % NT
    angles = phase_ids.astype(jnp.float32) * (2.0 * math.pi / NT)
    norm_scale = math.sqrt(2.0 / NT)
    return jnp.stack([jnp.cos(angles), -jnp.sin(angles)]) * norm_scale

def reference(kernel, tile_mask, direct, onsets):
    highest = lax.Precision.HIGHEST
    dft_table = phase_table()
    time_ids = jnp.arange(NT, dtype=jnp.int32)
    window = time_ids[None, None, :] < onsets[:, :, None]
    fields = jnp.einsum('rpt,kjt->kjrp', direct, dft_table, precision=highest).astype(jnp.bfloat16)
    focusing = direct
    for iteration in range(ITERS):

        def one_band(freq_index, current=fields):
            block_mask = jnp.repeat(jnp.repeat(tile_mask[freq_index], TILE, axis=0), TILE, axis=1).astype(jnp.bfloat16)
            real_kernel = (kernel[0, freq_index] * block_mask).astype(jnp.float32)
            imag_kernel = (kernel[1, freq_index] * block_mask).astype(jnp.float32)
            field_real = current[0, freq_index].astype(jnp.float32)
            field_imag = current[1, freq_index].astype(jnp.float32)
            out_real = jnp.dot(real_kernel, field_real, precision=highest) - jnp.dot(imag_kernel, field_imag, precision=highest)
            out_imag = jnp.dot(real_kernel, field_imag, precision=highest) + jnp.dot(imag_kernel, field_real, precision=highest)
            return jnp.stack([out_real, out_imag])
        bands = lax.map(one_band, jnp.arange(NF, dtype=jnp.int32))
        bands = jnp.transpose(bands, (1, 0, 2, 3)).astype(jnp.bfloat16)
        traces = jnp.einsum('kjrp,kjt->rpt', bands.astype(jnp.float32), dft_table, precision=highest)
        focusing = direct - jnp.where(window, traces, 0.0)
        if iteration + 1 < ITERS:
            fields = jnp.einsum('rpt,kjt->kjrp', focusing, dft_table, precision=highest).astype(jnp.bfloat16)
    return focusing
```

```python
import functools
import math

import jax
import jax.numpy as jnp
from jax import lax
from jax.experimental import pallas as pl
from jax.experimental.pallas import tpu as pltpu
from jax.sharding import PartitionSpec as P

NF = 128
NT = 512
TILE = 128
ITERS = 2
LANES = 128
CHUNKS = 2
GROUP = 16
SLOTS = 8
F32 = jnp.float32
BF16 = jnp.bfloat16
VMEM_LIMIT = 60 * 1024 * 1024


def phase_table():
    freq_ids = jnp.arange(NF, dtype=jnp.int32) + 1
    time_ids = jnp.arange(NT, dtype=jnp.int32)
    phase_ids = freq_ids[:, None] * time_ids[None, :] % NT
    angles = phase_ids.astype(F32) * (2.0 * math.pi / NT)
    norm_scale = math.sqrt(2.0 / NT)
    table = jnp.concatenate([jnp.cos(angles), -jnp.sin(angles)]) * norm_scale
    high = lax.reduce_precision(table, 8, 7)
    return high.astype(BF16), (table - high).astype(BF16)


def dot(a, b, dims=(1, 0)):
    return lax.dot_general(
        a, b, (((dims[0],), (dims[1],)), ((), ())), preferred_element_type=F32
    )


def split(x):
    high = x.astype(BF16)
    return high, (x - high.astype(F32)).astype(BF16)


def spectra_of(series, high_ref, low_ref, half, put, pair):
    s_high, s_low = split(series)
    t_high = high_ref[...]
    spectra = dot(t_high, s_high, (1, 1)) + dot(t_high, s_low, (1, 1)) + dot(low_ref[...], s_high, (1, 1))
    real, imag = spectra[:NF], spectra[NF:]
    left = lax.broadcasted_iota(jnp.int32, real.shape, 1) < half
    put(2 * pair, jnp.where(left, real, pltpu.roll(imag, half, 1)))
    put(2 * pair + 1, jnp.where(left, pltpu.roll(real, half, 1), imag))


def traces_of(get, high_ref, low_ref, half, pair):
    rows = []
    for which in range(2):
        turned = get(2 * pair + which).T
        rows.append(jnp.concatenate([turned[:half], turned[half:]], axis=1))
    stacked = jnp.concatenate(rows, axis=0).astype(BF16)
    return dot(stacked, high_ref[...]) + dot(stacked, low_ref[...])


def windowed(traces, onsets_ref, half, pair):
    onsets = onsets_ref[...]
    receiver = lax.broadcasted_iota(jnp.int32, onsets.shape, 1)
    first = pl.program_id(0) * GROUP + 2 * pair
    columns = [
        jnp.sum(jnp.where(receiver == first + which, onsets, 0), axis=1, keepdims=True)
        for which in range(2)
    ]
    ends = jnp.concatenate(columns, axis=0)
    times = lax.broadcasted_iota(jnp.int32, traces.shape, 1)
    return jnp.where(times < ends, traces, 0.0)


def strided(ref, row):
    return pl.ds(row, NF, stride=GROUP)


def store_out(out_ref, rows_ref):
    out_ref[...] = rows_ref[...].reshape(NF, GROUP, LANES).astype(BF16)


def first_kernel(direct_ref, high_ref, low_ref, out_ref, rows_ref, *, half):
    def put(row, value):
        rows_ref[strided(rows_ref, row), :] = value

    def step(pair, _):
        series = direct_ref[pl.ds(2 * pair, 2)].reshape(2 * half, NT)
        spectra_of(series, high_ref, low_ref, half, put, pair)
        return 0

    lax.fori_loop(0, GROUP // 2, step, 0)
    store_out(out_ref, rows_ref)


def middle_kernel(bands_ref, direct_ref, onsets_ref, high_ref, low_ref, out_ref, in_rows, rows_ref, *, half):
    in_rows[...] = bands_ref[...].astype(F32).reshape(NF * GROUP, LANES)

    def get(row):
        return in_rows[strided(in_rows, row), :]

    def put(row, value):
        rows_ref[strided(rows_ref, row), :] = value

    def step(pair, _):
        traces = traces_of(get, high_ref, low_ref, half, pair)
        series = direct_ref[pl.ds(2 * pair, 2)].reshape(2 * half, NT)
        series = series - windowed(traces, onsets_ref, half, pair)
        spectra_of(series, high_ref, low_ref, half, put, pair)
        return 0

    lax.fori_loop(0, GROUP // 2, step, 0)
    store_out(out_ref, rows_ref)


def last_kernel(bands_ref, direct_ref, onsets_ref, high_ref, low_ref, *rest, half):
    out_ref, in_rows = rest[-2:]
    in_rows[...] = bands_ref[...].astype(F32).reshape(NF * GROUP, LANES)

    def get(row):
        return in_rows[strided(in_rows, row), :]

    def step(pair, _):
        traces = traces_of(get, high_ref, low_ref, half, pair)
        series = direct_ref[pl.ds(2 * pair, 2)].reshape(2 * half, NT)
        series = series - windowed(traces, onsets_ref, half, pair)
        out_ref[pl.ds(2 * pair, 2)] = series.reshape(2, half, NT)
        return 0

    lax.fori_loop(0, GROUP // 2, step, 0)


def time_call(kind, chunk, receivers, focal, bands, direct, onsets, tables, out=None):
    half = focal // CHUNKS
    grid = (receivers // GROUP,)
    series_spec = pl.BlockSpec((GROUP, half, NT), lambda g: (g, chunk, 0))
    rows_spec = pl.BlockSpec((NF, GROUP, LANES), lambda g: (0, g, 0))
    onsets_spec = pl.BlockSpec((half, receivers), lambda g: (chunk, 0))
    table_spec = pl.BlockSpec((2 * NF, NT), lambda g: (0, 0))
    rows_scratch = pltpu.VMEM((NF * GROUP, LANES), F32)
    rows_shape = jax.ShapeDtypeStruct((NF, receivers, LANES), BF16)
    elements = receivers * half
    flops = 2 * elements * NT * 2 * NF
    series_bytes = elements * NT * 4
    params = pltpu.CompilerParams(vmem_limit_bytes=VMEM_LIMIT)
    if kind == "first":
        return pl.pallas_call(
            functools.partial(first_kernel, half=half),
            grid=grid,
            in_specs=[series_spec, table_spec, table_spec],
            out_specs=rows_spec,
            out_shape=rows_shape,
            scratch_shapes=[rows_scratch],
            compiler_params=params,
            cost_estimate=pl.CostEstimate(flops=3 * flops, bytes_accessed=2 * series_bytes, transcendentals=0),
            name=f"first_{chunk}",
        )(direct, *tables)
    if kind == "middle":
        return pl.pallas_call(
            functools.partial(middle_kernel, half=half),
            grid=grid,
            in_specs=[rows_spec, series_spec, onsets_spec, table_spec, table_spec],
            out_specs=rows_spec,
            out_shape=rows_shape,
            scratch_shapes=[rows_scratch, rows_scratch],
            compiler_params=params,
            cost_estimate=pl.CostEstimate(flops=5 * flops, bytes_accessed=2 * series_bytes, transcendentals=0),
            name=f"middle_{chunk}",
        )(bands, direct, onsets, *tables)
    operands = [bands, direct, onsets, *tables]
    specs = [rows_spec, series_spec, onsets_spec, table_spec, table_spec]
    aliases = {}
    if out is not None:
        aliases = {len(operands): 0}
        operands.append(out)
        specs.append(pl.BlockSpec(memory_space=pl.ANY))
    return pl.pallas_call(
        functools.partial(last_kernel, half=half),
        grid=grid,
        in_specs=specs,
        out_specs=series_spec,
        out_shape=jax.ShapeDtypeStruct(direct.shape, F32),
        scratch_shapes=[rows_scratch],
        input_output_aliases=aliases,
        compiler_params=params,
        cost_estimate=pl.CostEstimate(flops=2 * flops, bytes_accessed=3 * series_bytes, transcendentals=0),
        name=f"last_{chunk}",
    )(*operands)


def list_kernel(mask_ref, tiles_ref, starts_ref):
    freqs, row_tiles, column_tiles = mask_ref.shape

    def row(index, position):
        starts_ref[index] = position
        row_tile, freq = index // freqs, lax.rem(index, freqs)
        for column in range(column_tiles):
            tiles_ref[position] = index * column_tiles + column
            position = position + jnp.where(mask_ref[freq, row_tile, column] != 0, 1, 0)
        return position

    starts_ref[row_tiles * freqs] = lax.fori_loop(0, row_tiles * freqs, row, 0)


def list_call(tile_mask):
    freqs, row_tiles, column_tiles = tile_mask.shape
    smem = pl.BlockSpec(memory_space=pltpu.SMEM)
    return pl.pallas_call(
        list_kernel,
        in_specs=[smem],
        out_specs=[smem, smem],
        out_shape=[
            jax.ShapeDtypeStruct((freqs * row_tiles * column_tiles,), jnp.int32),
            jax.ShapeDtypeStruct((freqs * row_tiles + 1,), jnp.int32),
        ],
        name="list_tiles",
    )(tile_mask)


def product_kernel(tiles_ref, starts_ref, place_ref, kernel_ref, *rest, parts):
    field_refs, (out_ref, fields, slots, slot_sems, field_sems) = rest[:parts], rest[parts:]
    _, freqs, rows, columns = kernel_ref.shape
    owners, _, depth, lanes = out_ref.shape
    row_tiles, column_tiles = rows // TILE, columns // TILE
    per_tile = TILE // depth
    half = lanes // 2
    total = starts_ref[row_tiles * freqs]

    def tile_copy(index, slot):
        code = tiles_ref[index]
        column = lax.rem(code, column_tiles)
        line = code // column_tiles
        freq, row_tile = lax.rem(line, freqs), line // freqs
        return pltpu.make_async_copy(
            kernel_ref.at[:, freq, pl.ds(row_tile * TILE, TILE), pl.ds(column * TILE, TILE)],
            slots.at[slot],
            slot_sems.at[slot],
        )

    copies = [
        pltpu.make_async_copy(field_refs[part], fields.at[place_ref[part]], field_sems.at[part])
        for part in range(parts)
    ]
    for copy in copies:
        copy.start()
    for slot in range(SLOTS):

        @pl.when(slot < total)
        def _(slot=slot):
            tile_copy(slot, slot).start()

    for copy in copies:
        copy.wait()

    tiles_per_part = column_tiles // parts
    sign = jnp.where(lax.broadcasted_iota(jnp.int32, (TILE, lanes), 1) < half, -1.0, 1.0)

    def line_step(line, _):
        freq, row_tile = lax.rem(line, freqs), line // freqs

        def tile_step(index, total_sum):
            slot = lax.rem(index, SLOTS)
            tile_copy(index, slot).wait()
            column = lax.rem(tiles_ref[index], column_tiles)
            part, first = column // tiles_per_part, lax.rem(column, tiles_per_part) * per_tile
            field = fields[part, pl.ds(first, per_tile), freq].reshape(TILE, lanes)
            tile = slots[slot]
            both = jnp.concatenate([tile[0], tile[1]], axis=0)
            total_sum = total_sum + dot(both, field)

            @pl.when(index + SLOTS < total)
            def _():
                tile_copy(index + SLOTS, slot).start()

            return total_sum

        sums = lax.fori_loop(
            starts_ref[line], starts_ref[line + 1], tile_step, jnp.zeros((2 * TILE, lanes), F32)
        )
        bands = sums[:TILE] + sign * pltpu.roll(sums[TILE:], half, 1)
        bands = bands.astype(BF16).reshape(per_tile, depth, lanes)
        out_ref[pl.ds(row_tile * per_tile, per_tile), freq] = bands
        return 0

    lax.fori_loop(0, row_tiles * freqs, line_step, 0)


def product_call(chunk, tiles, starts, places, kernel, fields):
    owners, freqs, depth, lanes = fields[0].shape
    parts = len(fields)
    smem = pl.BlockSpec(memory_space=pltpu.SMEM)
    anywhere = pl.BlockSpec(memory_space=pl.ANY)
    return pl.pallas_call(
        functools.partial(product_kernel, parts=parts),
        in_specs=[smem, smem, smem, anywhere] + [anywhere] * parts,
        out_specs=pl.BlockSpec(memory_space=pltpu.VMEM),
        out_shape=jax.ShapeDtypeStruct(fields[0].shape, BF16),
        scratch_shapes=[
            pltpu.VMEM((parts,) + fields[0].shape, BF16),
            pltpu.VMEM((SLOTS, 2, TILE, TILE), BF16),
            pltpu.SemaphoreType.DMA((SLOTS,)),
            pltpu.SemaphoreType.DMA((parts,)),
        ],
        compiler_params=pltpu.CompilerParams(vmem_limit_bytes=VMEM_LIMIT),
        cost_estimate=pl.CostEstimate(
            flops=2 * kernel.size * lanes // 8, bytes_accessed=kernel.size // 4, transcendentals=0
        ),
        name=f"product_{chunk}",
    )(tiles, starts, places, kernel, *fields)


def to_freq(rows, owners):
    rows = rows.reshape((owners, rows.shape[0] // owners) + rows.shape[1:])
    return lax.all_to_all(rows, "freq", 0, 0, tiled=True)


def to_time(bands):
    rows = lax.all_to_all(bands, "freq", 0, 0, tiled=True)
    return rows.reshape((rows.shape[0] * rows.shape[1],) + rows.shape[2:])


def local(kernel, tile_mask, direct, onsets, *, owners, halves):
    receivers, focal, _ = direct.shape
    tables = phase_table()
    turned = onsets.T
    mine = lax.axis_index("rows")
    places = jnp.stack([lax.rem(mine - shift + halves, halves) for shift in range(halves)]).astype(jnp.int32)
    tiles, starts = list_call(tile_mask)

    def exchange(fields):
        got = [fields]
        for shift in range(1, halves):
            ring = [(place, (place + shift) % halves) for place in range(halves)]
            got.append(lax.ppermute(fields, "rows", ring))
        return got

    rows = [
        time_call("first", chunk, receivers, focal, None, direct, None, tables) for chunk in range(CHUNKS)
    ]
    out = None
    for iteration in range(ITERS):
        fields = [to_freq(rows[chunk], owners) for chunk in range(CHUNKS)]
        fields = [exchange(fields[chunk]) for chunk in range(CHUNKS)]
        bands = [
            product_call(chunk, tiles, starts, places, kernel, fields[chunk]) for chunk in range(CHUNKS)
        ]
        bands = [to_time(bands[chunk]) for chunk in range(CHUNKS)]
        if iteration + 1 < ITERS:
            rows = [
                time_call("middle", chunk, receivers, focal, bands[chunk], direct, turned, tables)
                for chunk in range(CHUNKS)
            ]
        else:
            for chunk in range(CHUNKS):
                out = time_call("last", chunk, receivers, focal, bands[chunk], direct, turned, tables, out)
    return out


def solution(mesh):
    return jax.shard_map(
        functools.partial(local, owners=mesh.shape["freq"], halves=mesh.shape["rows"]),
        mesh=mesh,
        in_specs=(
            P(None, "freq", "rows", None),
            P("freq", "rows", None),
            P(("rows", "freq"), None, None),
            P(("rows", "freq"), None),
        ),
        out_specs=P(("rows", "freq"), None, None),
        check_vma=False,
    )
```

```python
import functools
import math

import jax
import jax.numpy as jnp
from jax import lax
from jax.experimental import pallas as pl
from jax.experimental.pallas import tpu as pltpu
from jax.sharding import PartitionSpec as P


NF = 128
NT = 512
TILE = 128
ITERS = 2
LANES = 128
CHUNKS = 2
GROUP = 16
QUAD = 4
SLOTS = 4
BATCH = 8
PARTS = 2
F32 = jnp.float32
BF16 = jnp.bfloat16
VMEM_LIMIT = 60 * 1024 * 1024


def phase_tables():
    freq_ids = jnp.arange(NF, dtype=jnp.int32) + 1
    time_ids = jnp.arange(NT // 2, dtype=jnp.int32)
    phase_ids = freq_ids[:, None] * time_ids[None, :] % NT
    angles = phase_ids.astype(F32) * (2.0 * math.pi / NT)
    norm_scale = math.sqrt(2.0 / NT)
    table = jnp.stack([jnp.cos(angles), -jnp.sin(angles)]) * norm_scale
    table = table.reshape(2, NF // 2, 2, NT // 2).transpose(2, 0, 1, 3).reshape(2, NF, NT // 2)
    high = lax.reduce_precision(table, 8, 7)
    return jnp.concatenate([high, table - high], axis=1).astype(BF16)


def dot(a, b, dims=(1, 0)):
    return lax.dot_general(
        a, b, (((dims[0],), (dims[1],)), ((), ())), preferred_element_type=F32
    )


def split(x):
    high = x.astype(BF16)
    return high, (x - high.astype(F32)).astype(BF16)


def parity_rows(parity, receiver):
    return pl.ds(parity * GROUP + receiver, NF // 2, stride=2 * GROUP)


def to_rows(series, tables_ref, rows_ref, half, first):
    early, late = series[:, : NT // 2], series[:, NT // 2 :]
    for parity, folded in ((0, early - late), (1, early + late)):
        high, low = split(folded)
        both = dot(tables_ref[parity], high, (1, 1))
        spectra = both[:NF] + both[NF:] + dot(tables_ref[parity, :NF], low, (1, 1))
        for place in range(QUAD * half // LANES):
            pair = spectra[:, place * LANES : (place + 1) * LANES]
            real, imag = pair[: NF // 2], pair[NF // 2 :]
            left = lax.broadcasted_iota(jnp.int32, real.shape, 1) < half
            rows_ref[parity_rows(parity, first + 2 * place), :] = jnp.where(
                left, real, pltpu.roll(imag, half, 1)
            )
            rows_ref[parity_rows(parity, first + 2 * place + 1), :] = jnp.where(
                left, pltpu.roll(real, half, 1), imag
            )


def to_traces(rows_ref, tables_ref, half, first):
    odd, even = [], []
    for receiver in range(first, first + QUAD):
        rows = [rows_ref[parity_rows(parity, receiver), :] for parity in range(2)]
        turned = jnp.concatenate(rows, axis=0).T
        real, imag = turned[:half], turned[half:]
        left = lax.broadcasted_iota(jnp.int32, real.shape, 1) < NF // 2
        odd.append(jnp.where(left, real, pltpu.roll(imag, NF // 2, 1)))
        even.append(jnp.where(left, pltpu.roll(real, NF // 2, 1), imag))
    parts = []
    for parity, spectra in enumerate((odd, even)):
        spectra = jnp.concatenate(spectra, axis=0).astype(BF16)
        parts.append(dot(jnp.concatenate([spectra, spectra], axis=1), tables_ref[parity]))
    odd, even = parts
    return jnp.concatenate([even + odd, even - odd], axis=1)


def subtracted(direct_ref, traces, onsets_ref, half, first):
    series = direct_ref[first : first + QUAD].reshape(QUAD * half, NT)
    columns = [onsets_ref[0, :, first + which : first + which + 1] for which in range(QUAD)]
    ends = jnp.concatenate(columns, axis=0)
    times = lax.broadcasted_iota(jnp.int32, traces.shape, 1)
    return series - jnp.where(times < ends, traces, 0.0)


def store_out(out_ref, rows_ref):
    out_ref[...] = rows_ref[...].reshape(out_ref.shape).astype(BF16)


def load_in(rows_ref, bands_ref):
    rows_ref[...] = bands_ref[...].astype(F32).reshape(NF * GROUP, LANES)


def first_kernel(direct_ref, tables_ref, out_ref, rows_ref, *, half):
    for first in range(0, GROUP, QUAD):
        series = direct_ref[first : first + QUAD].reshape(QUAD * half, NT)
        to_rows(series, tables_ref, rows_ref, half, first)
    store_out(out_ref, rows_ref)


def middle_kernel(direct_ref, tables_ref, onsets_ref, bands_ref, out_ref, in_rows, rows_ref, *, half):
    load_in(in_rows, bands_ref)
    for first in range(0, GROUP, QUAD):
        traces = to_traces(in_rows, tables_ref, half, first)
        series = subtracted(direct_ref, traces, onsets_ref, half, first)
        to_rows(series, tables_ref, rows_ref, half, first)
    store_out(out_ref, rows_ref)


def last_kernel(direct_ref, tables_ref, onsets_ref, bands_ref, *rest, half):
    out_ref, in_rows = rest[-2:]
    load_in(in_rows, bands_ref)
    for first in range(0, GROUP, QUAD):
        traces = to_traces(in_rows, tables_ref, half, first)
        series = subtracted(direct_ref, traces, onsets_ref, half, first)
        out_ref[first : first + QUAD] = series.reshape(QUAD, half, NT)


def time_call(kind, chunk, owners, direct, tables, onsets=None, bands=None, out=None):
    receivers, focal, _ = direct.shape
    half = focal // CHUNKS
    freqs = NF // owners
    series_spec = pl.BlockSpec((GROUP, half, NT), lambda g: (g, chunk, 0))
    rows_spec = pl.BlockSpec((owners, freqs, GROUP, LANES), lambda g: (0, 0, g, 0))
    operands = [direct, tables]
    specs = [series_spec, pl.BlockSpec((2, 2 * NF, NT // 2), lambda g: (0, 0, 0))]
    if kind != "first":
        operands += [onsets, bands]
        specs += [pl.BlockSpec((1, half, GROUP), lambda g: (g, chunk, 0)), rows_spec]
    aliases = {}
    if out is not None:
        aliases = {len(operands): 0}
        operands.append(out)
        specs.append(pl.BlockSpec(memory_space=pl.ANY))
    rows_scratch = pltpu.VMEM((NF * GROUP, LANES), F32)
    if kind == "last":
        out_specs, out_shape = series_spec, jax.ShapeDtypeStruct(direct.shape, F32)
    else:
        out_specs = rows_spec
        out_shape = jax.ShapeDtypeStruct((owners, freqs, receivers, LANES), BF16)
    body, passes, scratches = {
        "first": (first_kernel, 3, 1),
        "middle": (middle_kernel, 5, 2),
        "last": (last_kernel, 2, 1),
    }[kind]
    elements = receivers * half * NT
    return pl.pallas_call(
        functools.partial(body, half=half),
        grid=(receivers // GROUP,),
        in_specs=specs,
        out_specs=out_specs,
        out_shape=out_shape,
        scratch_shapes=[rows_scratch] * scratches,
        input_output_aliases=aliases,
        compiler_params=pltpu.CompilerParams(vmem_limit_bytes=VMEM_LIMIT),
        cost_estimate=pl.CostEstimate(
            flops=4 * passes * elements * NF, bytes_accessed=8 * elements, transcendentals=0
        ),
    )(*operands)


def list_kernel(mask_ref, tiles_ref, count_ref):
    freqs, row_tiles, column_tiles = mask_ref.shape
    lines = row_tiles * freqs // PARTS
    for part in range(PARTS):
        base = part * (lines * column_tiles + BATCH)

        def row(line, position, part=part):
            row_tile, freq = line // (freqs // PARTS), lax.rem(line, freqs // PARTS)
            for column in range(column_tiles):
                tiles_ref[position] = line * column_tiles + column
                kept = mask_ref[part * (freqs // PARTS) + freq, row_tile, column] != 0
                position = position + jnp.where(kept, 1, 0)
            return position

        total = lax.fori_loop(0, lines, row, base)
        for extra in range(BATCH):
            tiles_ref[total + extra] = lines * column_tiles
        count_ref[part] = (total - base + BATCH - 1) // BATCH


def list_call(tile_mask):
    freqs, row_tiles, column_tiles = tile_mask.shape
    smem = pl.BlockSpec(memory_space=pltpu.SMEM)
    return pl.pallas_call(
        list_kernel,
        in_specs=[smem],
        out_specs=[smem, smem],
        out_shape=[
            jax.ShapeDtypeStruct((freqs * row_tiles * column_tiles + PARTS * BATCH,), jnp.int32),
            jax.ShapeDtypeStruct((PARTS,), jnp.int32),
        ],
        name="list_tiles",
    )(tile_mask)


def product_kernel(tiles_ref, count_ref, place_ref, kernel_ref, *rest, which_part, parts):
    field_refs, (out_ref, fields, sums, slots, slot_sems, field_sems) = rest[:parts], rest[-6:]
    _, _, rows, columns = kernel_ref.shape
    _, freqs, depth, lanes = out_ref.shape
    row_tiles, column_tiles = rows // TILE, columns // TILE
    lines = row_tiles * freqs
    per_tile = TILE // depth
    tiles_per_part = column_tiles // parts
    half = lanes // 2
    batches = count_ref[which_part]
    base = which_part * (lines * column_tiles + BATCH)

    def tile_copy(batch, which):
        code = tiles_ref[base + batch * BATCH + which]
        column = lax.rem(code, column_tiles)
        line = jnp.minimum(code // column_tiles, lines - 1)
        freq, row_tile = lax.rem(line, freqs), line // freqs
        slot = lax.rem(batch, SLOTS)
        return pltpu.make_async_copy(
            kernel_ref.at[:, which_part * freqs + freq, pl.ds(row_tile * TILE, TILE), pl.ds(column * TILE, TILE)],
            slots.at[slot, which],
            slot_sems.at[slot, which],
        )

    def start(batch):
        @pl.when(batch < batches)
        def _():
            for which in range(BATCH):
                tile_copy(batch, which).start()

    sources = [field_refs[0].at[:, pl.ds(which_part * freqs, freqs)], *field_refs[1:]]
    copies = [
        pltpu.make_async_copy(sources[part], fields.at[place_ref[part]], field_sems.at[part])
        for part in range(parts)
    ]
    for copy in copies:
        copy.start()
    for batch in range(SLOTS - 1):
        start(batch)

    def clear(line, _):
        sums[line] = jnp.zeros((TILE, lanes), F32)
        return 0

    lax.fori_loop(0, lines, clear, 0)
    for copy in copies:
        copy.wait()

    left = lax.broadcasted_iota(jnp.int32, (TILE, lanes), 1) < half

    def batch_step(batch, _):
        start(batch + SLOTS - 1)
        slot = lax.rem(batch, SLOTS)
        results = []
        for which in range(BATCH):
            tile_copy(batch, which).wait()
        for which in range(BATCH):
            code = tiles_ref[base + batch * BATCH + which]
            column, line = lax.rem(code, column_tiles), code // column_tiles
            part, first = column // tiles_per_part, lax.rem(column, tiles_per_part) * per_tile
            field = fields[part, pl.ds(first, per_tile), lax.rem(line, freqs)].reshape(TILE, lanes)
            swapped = pltpu.roll(field.astype(F32), half, 1)
            swapped = jnp.where(left, -swapped, swapped).astype(BF16)
            both = jnp.concatenate([slots[slot, which, 0], slots[slot, which, 1]], axis=1)
            results.append((line, dot(both, jnp.concatenate([field, swapped], axis=0))))
        for line, result in results:
            sums[line] += result
        return 0

    lax.fori_loop(0, batches, batch_step, 0)

    def finish(line, _):
        freq, row_tile = lax.rem(line, freqs), line // freqs
        bands = sums[line].astype(BF16).reshape(per_tile, depth, lanes)
        out_ref[pl.ds(row_tile * per_tile, per_tile), freq] = bands
        return 0

    lax.fori_loop(0, lines, finish, 0)


def product_call(part, tiles, count, places, kernel, fields, out):
    owners, freqs, depth, lanes = fields[0].shape
    freqs = freqs // PARTS
    lines = kernel.shape[2] // TILE * freqs
    parts = len(fields)
    smem = pl.BlockSpec(memory_space=pltpu.SMEM)
    anywhere = pl.BlockSpec(memory_space=pl.ANY)
    operands = [tiles, count, places, kernel, *fields]
    aliases = {}
    if out is not None:
        aliases = {len(operands): 0}
        operands.append(out)
    return pl.pallas_call(
        functools.partial(product_kernel, which_part=part, parts=parts),
        grid=(1,),
        in_specs=[smem, smem, smem] + [anywhere] * (len(operands) - 3),
        out_specs=pl.BlockSpec((owners, freqs, depth, lanes), lambda g: (0, part, 0, 0)),
        out_shape=jax.ShapeDtypeStruct(fields[0].shape, BF16),
        scratch_shapes=[
            pltpu.VMEM((parts, owners, freqs, depth, lanes), BF16),
            pltpu.VMEM((lines + 1, TILE, lanes), F32),
            pltpu.VMEM((SLOTS, BATCH, 2, TILE, TILE), BF16),
            pltpu.SemaphoreType.DMA((SLOTS, BATCH)),
            pltpu.SemaphoreType.DMA((parts,)),
        ],
        input_output_aliases=aliases,
        compiler_params=pltpu.CompilerParams(vmem_limit_bytes=VMEM_LIMIT),
        cost_estimate=pl.CostEstimate(
            flops=2 * kernel.size * lanes // 8 // PARTS,
            bytes_accessed=kernel.size // 4 // PARTS,
            transcendentals=0,
        ),
    )(*operands)


def local(kernel, tile_mask, direct, onsets, *, owners, halves):
    receivers, focal, _ = direct.shape
    tables = phase_tables()
    onsets = onsets.reshape(receivers // GROUP, GROUP, focal).transpose(0, 2, 1)
    mine = lax.axis_index("rows")
    places = jnp.stack([lax.rem(mine - shift + halves, halves) for shift in range(halves)]).astype(jnp.int32)
    tiles, count = list_call(tile_mask)

    def across(rows):
        return lax.all_to_all(rows, "freq", 0, 0, tiled=True)

    def exchange(fields, part):
        freqs = fields.shape[1] // PARTS
        piece = lax.slice_in_dim(fields, part * freqs, (part + 1) * freqs, axis=1)
        got = [fields]
        for shift in range(1, halves):
            ring = [(place, (place + shift) % halves) for place in range(halves)]
            got.append(lax.ppermute(piece, "rows", ring))
        return got

    def time_at(kind, chunk, *operands):
        return time_call(kind, chunk, owners, direct, tables, *operands)

    rows = [time_at("first", chunk) for chunk in range(CHUNKS)]
    out = None
    for turn in range(ITERS):
        bands = [None] * CHUNKS
        for chunk in range(CHUNKS):
            fields = across(rows[chunk])
            for part in range(PARTS):
                both = exchange(fields, part)
                bands[chunk] = product_call(part, tiles, count, places, kernel, both, bands[chunk])
        bands = [across(bands[chunk]) for chunk in range(CHUNKS)]
        for chunk in range(CHUNKS):
            if turn + 1 < ITERS:
                rows[chunk] = time_at("middle", chunk, onsets, bands[chunk])
            else:
                out = time_at("last", chunk, onsets, bands[chunk], out)
    return out


def solution(mesh):
    owners, halves = mesh.shape["freq"], mesh.shape["rows"]
    return jax.shard_map(
        functools.partial(local, owners=owners, halves=halves),
        mesh=mesh,
        in_specs=(
            P(None, "freq", "rows", None),
            P("freq", "rows", None),
            P(("rows", "freq"), None, None),
            P(("rows", "freq"), None),
        ),
        out_specs=P(("rows", "freq"), None, None),
        check_vma=False,
    )
```

```python
import functools
import math

import jax
import jax.numpy as jnp
from jax import lax
from jax.experimental import pallas as pl
from jax.experimental.pallas import tpu as pltpu
from jax.sharding import PartitionSpec as P


NF = 128
NT = 512
TILE = 128
ITERS = 2
LANES = 128
CHUNKS = 2
GROUP = 16
QUAD = 4
SLOTS = 4
BATCH = 8
REACHES = 2
F32 = jnp.float32
BF16 = jnp.bfloat16
VMEM_LIMIT = 60 * 1024 * 1024


def phase_tables():
    freq_ids = jnp.arange(NF, dtype=jnp.int32) + 1
    time_ids = jnp.arange(NT // 2, dtype=jnp.int32)
    phase_ids = freq_ids[:, None] * time_ids[None, :] % NT
    angles = phase_ids.astype(F32) * (2.0 * math.pi / NT)
    norm_scale = math.sqrt(2.0 / NT)
    table = jnp.stack([jnp.cos(angles), -jnp.sin(angles)]) * norm_scale
    table = table.reshape(2, NF // 2, 2, NT // 2).transpose(2, 0, 1, 3).reshape(2, NF, NT // 2)
    high = lax.reduce_precision(table, 8, 7)
    return jnp.concatenate([high, table - high], axis=1).astype(BF16)


def dot(a, b, dims=(1, 0)):
    return lax.dot_general(
        a, b, (((dims[0],), (dims[1],)), ((), ())), preferred_element_type=F32
    )


def split(x):
    high = x.astype(BF16)
    return high, (x - high.astype(F32)).astype(BF16)


def parity_rows(parity, receiver):
    return pl.ds(parity * GROUP + receiver, NF // 2, stride=2 * GROUP)


def to_rows(series, tables_ref, rows_ref, half, first):
    early, late = series[:, : NT // 2], series[:, NT // 2 :]
    for parity, folded in ((0, early - late), (1, early + late)):
        high, low = split(folded)
        both = dot(tables_ref[parity], high, (1, 1))
        spectra = both[:NF] + both[NF:] + dot(tables_ref[parity, :NF], low, (1, 1))
        for place in range(QUAD * half // LANES):
            pair = spectra[:, place * LANES : (place + 1) * LANES]
            real, imag = pair[: NF // 2], pair[NF // 2 :]
            left = lax.broadcasted_iota(jnp.int32, real.shape, 1) < half
            rows_ref[parity_rows(parity, first + 2 * place), :] = jnp.where(
                left, real, pltpu.roll(imag, half, 1)
            )
            rows_ref[parity_rows(parity, first + 2 * place + 1), :] = jnp.where(
                left, pltpu.roll(real, half, 1), imag
            )


def to_traces(rows_ref, tables_ref, half, first):
    odd, even = [], []
    for receiver in range(first, first + QUAD):
        rows = [rows_ref[parity_rows(parity, receiver), :] for parity in range(2)]
        turned = jnp.concatenate(rows, axis=0).T
        real, imag = turned[:half], turned[half:]
        left = lax.broadcasted_iota(jnp.int32, real.shape, 1) < NF // 2
        odd.append(jnp.where(left, real, pltpu.roll(imag, NF // 2, 1)))
        even.append(jnp.where(left, pltpu.roll(real, NF // 2, 1), imag))
    parts = []
    for parity, spectra in enumerate((odd, even)):
        spectra = jnp.concatenate(spectra, axis=0).astype(BF16)
        parts.append(dot(jnp.concatenate([spectra, spectra], axis=1), tables_ref[parity]))
    odd, even = parts
    return jnp.concatenate([even + odd, even - odd], axis=1)


def subtracted(direct_ref, traces, onsets_ref, half, first):
    series = direct_ref[first : first + QUAD].reshape(QUAD * half, NT)
    columns = [onsets_ref[0, :, first + which : first + which + 1] for which in range(QUAD)]
    ends = jnp.concatenate(columns, axis=0)
    times = lax.broadcasted_iota(jnp.int32, traces.shape, 1)
    return series - jnp.where(times < ends, traces, 0.0)


def store_out(out_refs, rows_ref, mine):
    for shift, out_ref in enumerate(out_refs):
        owner = lax.bitwise_xor(mine, shift)
        size = NF // len(out_refs) * GROUP
        rows = rows_ref[pl.ds(pl.multiple_of(owner * size, size), size), :]
        out_ref[...] = rows.reshape(out_ref.shape).astype(BF16)


def load_in(rows_ref, bands_ref):
    rows_ref[...] = bands_ref[...].astype(F32).reshape(NF * GROUP, LANES)


def first_kernel(mine_ref, direct_ref, tables_ref, *rest, half):
    out_refs, rows_ref = rest[:-1], rest[-1]
    for first in range(0, GROUP, QUAD):
        series = direct_ref[first : first + QUAD].reshape(QUAD * half, NT)
        to_rows(series, tables_ref, rows_ref, half, first)
    store_out(out_refs, rows_ref, mine_ref[0])


def middle_kernel(mine_ref, direct_ref, tables_ref, onsets_ref, bands_ref, *rest, half):
    out_refs, (in_rows, rows_ref) = rest[:-2], rest[-2:]
    load_in(in_rows, bands_ref)
    for first in range(0, GROUP, QUAD):
        traces = to_traces(in_rows, tables_ref, half, first)
        series = subtracted(direct_ref, traces, onsets_ref, half, first)
        to_rows(series, tables_ref, rows_ref, half, first)
    store_out(out_refs, rows_ref, mine_ref[0])


def last_kernel(mine_ref, direct_ref, tables_ref, onsets_ref, bands_ref, *rest, half):
    out_ref, in_rows = rest[-2:]
    load_in(in_rows, bands_ref)
    for first in range(0, GROUP, QUAD):
        traces = to_traces(in_rows, tables_ref, half, first)
        series = subtracted(direct_ref, traces, onsets_ref, half, first)
        out_ref[first : first + QUAD] = series.reshape(QUAD, half, NT)


def time_call(kind, chunk, owners, mine, direct, tables, onsets=None, bands=None, out=None):
    receivers, focal, _ = direct.shape
    half = focal // CHUNKS
    freqs = NF // owners
    series_spec = pl.BlockSpec((GROUP, half, NT), lambda g: (g, chunk, 0))
    rows_spec = pl.BlockSpec((owners, freqs, GROUP, LANES), lambda g: (0, 0, g, 0))
    operands = [mine, direct, tables]
    specs = [pl.BlockSpec(memory_space=pltpu.SMEM), series_spec, pl.BlockSpec((2, 2 * NF, NT // 2), lambda g: (0, 0, 0))]
    if kind != "first":
        operands += [onsets, bands]
        specs += [pl.BlockSpec((1, half, GROUP), lambda g: (g, chunk, 0)), rows_spec]
    aliases = {}
    if out is not None:
        aliases = {len(operands): 0}
        operands.append(out)
        specs.append(pl.BlockSpec(memory_space=pl.ANY))
    rows_scratch = pltpu.VMEM((NF * GROUP, LANES), F32)
    if kind == "last":
        out_specs, out_shape = series_spec, jax.ShapeDtypeStruct(direct.shape, F32)
    else:
        out_specs = [pl.BlockSpec((freqs, GROUP, LANES), lambda g: (0, g, 0))] * owners
        out_shape = [jax.ShapeDtypeStruct((freqs, receivers, LANES), BF16)] * owners
    body, passes, scratches = {
        "first": (first_kernel, 3, 1),
        "middle": (middle_kernel, 5, 2),
        "last": (last_kernel, 2, 1),
    }[kind]
    elements = receivers * half * NT
    return pl.pallas_call(
        functools.partial(body, half=half),
        grid=(receivers // GROUP,),
        in_specs=specs,
        out_specs=out_specs,
        out_shape=out_shape,
        scratch_shapes=[rows_scratch] * scratches,
        input_output_aliases=aliases,
        compiler_params=pltpu.CompilerParams(vmem_limit_bytes=VMEM_LIMIT),
        cost_estimate=pl.CostEstimate(
            flops=4 * passes * elements * NF, bytes_accessed=8 * elements, transcendentals=0
        ),
    )(*operands)


def list_kernel(mask_ref, tiles_ref, count_ref):
    freqs, row_tiles, column_tiles = mask_ref.shape
    lines = row_tiles * freqs

    def row(line, position):
        row_tile, freq = line // freqs, lax.rem(line, freqs)
        for column in range(column_tiles):
            tiles_ref[position] = line * column_tiles + column
            position = position + jnp.where(mask_ref[freq, row_tile, column] != 0, 1, 0)
        return position

    total = lax.fori_loop(0, lines, row, 0)
    for extra in range(BATCH):
        tiles_ref[total + extra] = lines * column_tiles
    count_ref[0] = (total + BATCH - 1) // BATCH


def list_call(tile_mask):
    freqs, row_tiles, column_tiles = tile_mask.shape
    smem = pl.BlockSpec(memory_space=pltpu.SMEM)
    return pl.pallas_call(
        list_kernel,
        in_specs=[smem],
        out_specs=[smem, smem],
        out_shape=[
            jax.ShapeDtypeStruct((freqs * row_tiles * column_tiles + BATCH,), jnp.int32),
            jax.ShapeDtypeStruct((1,), jnp.int32),
        ],
        name="list_tiles",
    )(tile_mask)


def product_kernel(tiles_ref, count_ref, place_ref, kernel_ref, *rest, parts):
    field_refs, (out_ref, fields, sums, slots, slot_sems, field_sems) = rest[:-6], rest[-6:]
    _, _, rows, columns = kernel_ref.shape
    _, freqs, depth, lanes = out_ref.shape
    row_tiles, column_tiles = rows // TILE, columns // TILE
    lines = row_tiles * freqs
    per_tile = TILE // depth
    tiles_per_part = column_tiles // parts
    half = lanes // 2
    batches = count_ref[0]

    def tile_copy(batch, which):
        code = tiles_ref[batch * BATCH + which]
        column = lax.rem(code, column_tiles)
        line = jnp.minimum(code // column_tiles, lines - 1)
        freq, row_tile = lax.rem(line, freqs), line // freqs
        slot = lax.rem(batch, SLOTS)
        return pltpu.make_async_copy(
            kernel_ref.at[:, freq, pl.ds(row_tile * TILE, TILE), pl.ds(column * TILE, TILE)],
            slots.at[slot, which],
            slot_sems.at[slot, which],
        )

    def start(batch):
        @pl.when(batch < batches)
        def _():
            for which in range(BATCH):
                tile_copy(batch, which).start()

    mine = place_ref[parts]
    groups = len(field_refs) // parts
    copies = []
    for index, field_ref in enumerate(field_refs):
        part, group = index // groups, index % groups
        size = field_ref.shape[0]
        target = fields.at[place_ref[part], pl.ds(group * size, size)]
        copies.append(pltpu.make_async_copy(field_ref, target, field_sems.at[index]))
    for copy in copies:
        copy.start()
    for batch in range(SLOTS - 1):
        start(batch)

    def clear(line, _):
        sums[line] = jnp.zeros((TILE, lanes), F32)
        return 0

    lax.fori_loop(0, lines, clear, 0)
    for copy in copies:
        copy.wait()

    left = lax.broadcasted_iota(jnp.int32, (TILE, lanes), 1) < half

    def batch_step(batch, _):
        start(batch + SLOTS - 1)
        slot = lax.rem(batch, SLOTS)
        results = []
        for which in range(BATCH):
            tile_copy(batch, which).wait()
        for which in range(BATCH):
            code = tiles_ref[batch * BATCH + which]
            column, line = lax.rem(code, column_tiles), code // column_tiles
            part, first = column // tiles_per_part, lax.rem(column, tiles_per_part) * per_tile
            freq = lax.rem(line, freqs)
            field = [fields[part, lax.bitwise_xor(first + k, mine), freq] for k in range(per_tile)]
            field = jnp.concatenate(field, axis=0)
            swapped = pltpu.roll(field.astype(F32), half, 1)
            swapped = jnp.where(left, -swapped, swapped).astype(BF16)
            both = jnp.concatenate([slots[slot, which, 0], slots[slot, which, 1]], axis=1)
            results.append((line, dot(both, jnp.concatenate([field, swapped], axis=0))))
        for line, result in results:
            sums[line] += result
        return 0

    lax.fori_loop(0, batches, batch_step, 0)

    def finish(line, _):
        freq, row_tile = lax.rem(line, freqs), line // freqs
        bands = sums[line].astype(BF16).reshape(per_tile, depth, lanes)
        out_ref[pl.ds(row_tile * per_tile, per_tile), freq] = bands
        return 0

    lax.fori_loop(0, lines, finish, 0)


def product_call(tiles, count, places, kernel, fields, parts):
    owners = sum(field.shape[0] for field in fields) // parts
    _, freqs, depth, lanes = fields[0].shape
    lines = kernel.shape[2] // TILE * freqs
    smem = pl.BlockSpec(memory_space=pltpu.SMEM)
    anywhere = pl.BlockSpec(memory_space=pl.ANY)
    return pl.pallas_call(
        functools.partial(product_kernel, parts=parts),
        in_specs=[smem, smem, smem, anywhere] + [anywhere] * len(fields),
        out_specs=pl.BlockSpec(memory_space=pltpu.VMEM),
        out_shape=jax.ShapeDtypeStruct((owners, freqs, depth, lanes), BF16),
        scratch_shapes=[
            pltpu.VMEM((parts, owners, freqs, depth, lanes), BF16),
            pltpu.VMEM((lines + 1, TILE, lanes), F32),
            pltpu.VMEM((SLOTS, BATCH, 2, TILE, TILE), BF16),
            pltpu.SemaphoreType.DMA((SLOTS, BATCH)),
            pltpu.SemaphoreType.DMA((len(fields),)),
        ],
        compiler_params=pltpu.CompilerParams(vmem_limit_bytes=VMEM_LIMIT),
        cost_estimate=pl.CostEstimate(
            flops=2 * kernel.size * lanes // 8, bytes_accessed=kernel.size // 4, transcendentals=0
        ),
    )(tiles, count, places, kernel, *fields)


def collect_kernel(*refs):
    blocks, (out_ref, sems) = refs[:-2], refs[-2:]
    copies = [
        pltpu.make_async_copy(block, out_ref.at[place], sems.at[place]) for place, block in enumerate(blocks)
    ]
    for copy in copies:
        copy.start()
    for copy in copies:
        copy.wait()


def collect_call(blocks):
    size = len(blocks) * blocks[0].size
    return pl.pallas_call(
        collect_kernel,
        in_specs=[pl.BlockSpec(memory_space=pl.ANY)] * len(blocks),
        out_specs=pl.BlockSpec(memory_space=pltpu.VMEM),
        out_shape=jax.ShapeDtypeStruct((len(blocks),) + blocks[0].shape, BF16),
        scratch_shapes=[pltpu.SemaphoreType.DMA((len(blocks),))],
        compiler_params=pltpu.CompilerParams(vmem_limit_bytes=VMEM_LIMIT),
        cost_estimate=pl.CostEstimate(flops=0, bytes_accessed=4 * size, transcendentals=0),
    )(*blocks)


def local(kernel, tile_mask, direct, onsets, *, owners, halves):
    receivers, focal, _ = direct.shape
    tables = phase_tables()
    onsets = onsets.reshape(receivers // GROUP, GROUP, focal).transpose(0, 2, 1)
    row, mine = lax.axis_index("rows"), lax.axis_index("freq").astype(jnp.int32)
    places = [lax.rem(row - shift + halves, halves) for shift in range(halves)]
    places = jnp.stack([*places, mine]).astype(jnp.int32)
    mine = mine[None]
    tiles, count = list_call(tile_mask)

    def time_at(kind, chunk, *operands):
        return time_call(kind, chunk, owners, mine, direct, tables, *operands)

    def spread(blocks):
        got = list(blocks)
        for shift in range(1, owners):
            pairs = [(place, place ^ shift) for place in range(owners)]
            got[shift] = lax.ppermute(blocks[shift], "freq", pairs)
        size = owners // REACHES
        fields = [[] for _ in range(halves)]
        for reach in range(REACHES):
            mine = collect_call(got[reach * size : (reach + 1) * size])
            fields[0].append(mine)
            for shift in range(1, halves):
                ring = [(place, (place + shift) % halves) for place in range(halves)]
                fields[shift].append(lax.ppermute(mine, "rows", ring))
        return [field for of_shift in fields for field in of_shift]

    def gather(bands):
        return lax.all_to_all(bands, "freq", 0, 0, tiled=True)

    blocks = [time_at("first", chunk) for chunk in range(CHUNKS)]
    out = None
    for turn in range(ITERS):
        bands = [None] * CHUNKS
        for chunk in range(CHUNKS):
            fields = spread(blocks[chunk])
            bands[chunk] = product_call(tiles, count, places, kernel, fields, halves)
        bands = [gather(bands[chunk]) for chunk in range(CHUNKS)]
        for chunk in range(CHUNKS):
            if turn + 1 < ITERS:
                blocks[chunk] = time_at("middle", chunk, onsets, bands[chunk])
            else:
                out = time_at("last", chunk, onsets, bands[chunk], out)
    return out


def solution(mesh):
    owners, halves = mesh.shape["freq"], mesh.shape["rows"]
    return jax.shard_map(
        functools.partial(local, owners=owners, halves=halves),
        mesh=mesh,
        in_specs=(
            P(None, "freq", "rows", None),
            P("freq", "rows", None),
            P(("rows", "freq"), None, None),
            P(("rows", "freq"), None),
        ),
        out_specs=P(("rows", "freq"), None, None),
        check_vma=False,
    )
```

```python
import functools
import math

import jax
import jax.numpy as jnp
from jax import lax
from jax.experimental import pallas as pl
from jax.experimental.pallas import tpu as pltpu
from jax.sharding import PartitionSpec as P


NF = 128
NT = 512
TILE = 128
ITERS = 2
LANES = 128
CHUNKS = 2
GROUP = 16
QUAD = 4
SLOTS = 3
BATCH = 16
REACHES = 2
F32 = jnp.float32
BF16 = jnp.bfloat16
VMEM_LIMIT = 24 * 1024 * 1024
TIME_VMEM_LIMIT = 50 * 1024 * 1024


def phase_tables():
    freq_ids = jnp.arange(NF, dtype=jnp.int32) + 1
    time_ids = jnp.arange(NT // 2, dtype=jnp.int32)
    phase_ids = freq_ids[:, None] * time_ids[None, :] % NT
    angles = phase_ids.astype(F32) * (2.0 * math.pi / NT)
    norm_scale = math.sqrt(2.0 / NT)
    table = jnp.stack([jnp.cos(angles), -jnp.sin(angles)]) * norm_scale
    table = table.reshape(2, NF // 2, 2, NT // 2).transpose(2, 0, 1, 3).reshape(2, NF, NT // 2)
    high = lax.reduce_precision(table, 8, 7)
    return jnp.concatenate([high, table - high], axis=1).astype(BF16)


def dot(a, b, dims=(1, 0)):
    return lax.dot_general(
        a, b, (((dims[0],), (dims[1],)), ((), ())), preferred_element_type=F32
    )


def split(x):
    high = x.astype(BF16)
    return high, (x - high.astype(F32)).astype(BF16)


def parity_rows(parity, receiver):
    return pl.ds(parity * GROUP + receiver, NF // 2, stride=2 * GROUP)


def to_rows(series, tables_ref, rows_ref, half, first):
    early, late = series[:, : NT // 2], series[:, NT // 2 :]
    for parity, folded in ((0, early - late), (1, early + late)):
        high, low = split(folded)
        both = dot(tables_ref[parity], high, (1, 1))
        spectra = both[:NF] + both[NF:] + dot(tables_ref[parity, :NF], low, (1, 1))
        for place in range(QUAD * half // LANES):
            pair = spectra[:, place * LANES : (place + 1) * LANES]
            real, imag = pair[: NF // 2], pair[NF // 2 :]
            left = lax.broadcasted_iota(jnp.int32, real.shape, 1) < half
            rows_ref[parity_rows(parity, first + 2 * place), :] = jnp.where(
                left, real, pltpu.roll(imag, half, 1)
            )
            rows_ref[parity_rows(parity, first + 2 * place + 1), :] = jnp.where(
                left, pltpu.roll(real, half, 1), imag
            )


def to_traces(rows_ref, tables_ref, half, first):
    odd, even = [], []
    for receiver in range(first, first + QUAD):
        rows = [rows_ref[parity_rows(parity, receiver), :] for parity in range(2)]
        turned = jnp.concatenate(rows, axis=0).T
        real, imag = turned[:half], turned[half:]
        left = lax.broadcasted_iota(jnp.int32, real.shape, 1) < NF // 2
        odd.append(jnp.where(left, real, pltpu.roll(imag, NF // 2, 1)))
        even.append(jnp.where(left, pltpu.roll(real, NF // 2, 1), imag))
    parts = []
    for parity, spectra in enumerate((odd, even)):
        spectra = jnp.concatenate(spectra, axis=0).astype(BF16)
        parts.append(dot(jnp.concatenate([spectra, spectra], axis=1), tables_ref[parity]))
    odd, even = parts
    return jnp.concatenate([even + odd, even - odd], axis=1)


def subtracted(direct_ref, traces, onsets_ref, half, first):
    series = direct_ref[first : first + QUAD].reshape(QUAD * half, NT)
    columns = [onsets_ref[0, :, first + which : first + which + 1] for which in range(QUAD)]
    ends = jnp.concatenate(columns, axis=0)
    times = lax.broadcasted_iota(jnp.int32, traces.shape, 1)
    return series - jnp.where(times < ends, traces, 0.0)


def store_out(out_refs, rows_ref, mine):
    for shift, out_ref in enumerate(out_refs):
        owner = lax.bitwise_xor(mine, shift)
        size = NF // len(out_refs) * GROUP
        rows = rows_ref[pl.ds(pl.multiple_of(owner * size, size), size), :]
        out_ref[...] = rows.reshape(out_ref.shape).astype(BF16)


def load_in(rows_ref, bands_ref):
    rows_ref[...] = bands_ref[...].astype(F32).reshape(NF * GROUP, LANES)


def first_kernel(mine_ref, direct_ref, tables_ref, *rest, half):
    out_refs, rows_ref = rest[:-1], rest[-1]
    for first in range(0, GROUP, QUAD):
        series = direct_ref[first : first + QUAD].reshape(QUAD * half, NT)
        to_rows(series, tables_ref, rows_ref, half, first)
    store_out(out_refs, rows_ref, mine_ref[0])


def middle_kernel(mine_ref, direct_ref, tables_ref, onsets_ref, bands_ref, *rest, half):
    out_refs, (in_rows, rows_ref) = rest[:-2], rest[-2:]
    load_in(in_rows, bands_ref)
    for first in range(0, GROUP, QUAD):
        traces = to_traces(in_rows, tables_ref, half, first)
        series = subtracted(direct_ref, traces, onsets_ref, half, first)
        to_rows(series, tables_ref, rows_ref, half, first)
    store_out(out_refs, rows_ref, mine_ref[0])


def last_kernel(mine_ref, direct_ref, tables_ref, onsets_ref, bands_ref, *rest, half):
    out_ref, in_rows = rest[-2:]
    load_in(in_rows, bands_ref)
    for first in range(0, GROUP, QUAD):
        traces = to_traces(in_rows, tables_ref, half, first)
        series = subtracted(direct_ref, traces, onsets_ref, half, first)
        out_ref[first : first + QUAD] = series.reshape(QUAD, half, NT)


def time_call(kind, chunk, owners, mine, direct, tables, onsets=None, bands=None, out=None):
    receivers, focal, _ = direct.shape
    half = focal // CHUNKS
    freqs = NF // owners
    series_spec = pl.BlockSpec((GROUP, half, NT), lambda g: (g, chunk, 0))
    rows_spec = pl.BlockSpec((owners, freqs, GROUP, LANES), lambda g: (0, 0, g, 0))
    operands = [mine, direct, tables]
    specs = [pl.BlockSpec(memory_space=pltpu.SMEM), series_spec, pl.BlockSpec((2, 2 * NF, NT // 2), lambda g: (0, 0, 0))]
    if kind != "first":
        operands += [onsets, bands]
        specs += [pl.BlockSpec((1, half, GROUP), lambda g: (g, chunk, 0)), rows_spec]
    aliases = {}
    if out is not None:
        aliases = {len(operands): 0}
        operands.append(out)
        specs.append(pl.BlockSpec(memory_space=pl.ANY))
    rows_scratch = pltpu.VMEM((NF * GROUP, LANES), F32)
    if kind == "last":
        out_specs, out_shape = series_spec, jax.ShapeDtypeStruct(direct.shape, F32)
    else:
        out_specs = [pl.BlockSpec((freqs, GROUP, LANES), lambda g: (0, g, 0))] * owners
        out_shape = [jax.ShapeDtypeStruct((freqs, receivers, LANES), BF16)] * owners
    body, passes, scratches = {
        "first": (first_kernel, 3, 1),
        "middle": (middle_kernel, 5, 2),
        "last": (last_kernel, 2, 1),
    }[kind]
    elements = receivers * half * NT
    return pl.pallas_call(
        functools.partial(body, half=half),
        grid=(receivers // GROUP,),
        in_specs=specs,
        out_specs=out_specs,
        out_shape=out_shape,
        scratch_shapes=[rows_scratch] * scratches,
        input_output_aliases=aliases,
        compiler_params=pltpu.CompilerParams(vmem_limit_bytes=TIME_VMEM_LIMIT),
        cost_estimate=pl.CostEstimate(
            flops=4 * passes * elements * NF, bytes_accessed=8 * elements, transcendentals=0
        ),
    )(*operands)


def list_kernel(mask_ref, tiles_ref, count_ref):
    freqs, row_tiles, column_tiles = mask_ref.shape
    lines = row_tiles * freqs

    def row(line, position):
        row_tile, freq = line // freqs, lax.rem(line, freqs)
        for column in range(column_tiles):
            tiles_ref[position] = line * column_tiles + column
            position = position + jnp.where(mask_ref[freq, row_tile, column] != 0, 1, 0)
        return position

    total = lax.fori_loop(0, lines, row, 0)
    for extra in range(BATCH):
        tiles_ref[total + extra] = lines * column_tiles
    count_ref[0] = (total + BATCH - 1) // BATCH


def list_call(tile_mask):
    freqs, row_tiles, column_tiles = tile_mask.shape
    smem = pl.BlockSpec(memory_space=pltpu.SMEM)
    return pl.pallas_call(
        list_kernel,
        in_specs=[smem],
        out_specs=[smem, smem],
        out_shape=[
            jax.ShapeDtypeStruct((freqs * row_tiles * column_tiles + BATCH,), jnp.int32),
            jax.ShapeDtypeStruct((1,), jnp.int32),
        ],
        compiler_params=pltpu.CompilerParams(vmem_limit_bytes=1024 * 1024),
        name="list_tiles",
    )(tile_mask)


def product_kernel(tiles_ref, count_ref, place_ref, kernel_ref, *rest, parts):
    field_refs, (out_ref, fields, sums, slots, slot_sems, field_sems) = rest[:-6], rest[-6:]
    _, _, rows, columns = kernel_ref.shape
    _, freqs, depth, lanes = out_ref.shape
    row_tiles, column_tiles = rows // TILE, columns // TILE
    lines = row_tiles * freqs
    per_tile = TILE // depth
    tiles_per_part = column_tiles // parts
    half = lanes // 2
    batches = count_ref[0]

    def tile_copy(batch, which):
        code = tiles_ref[batch * BATCH + which]
        column = lax.rem(code, column_tiles)
        line = jnp.minimum(code // column_tiles, lines - 1)
        freq, row_tile = lax.rem(line, freqs), line // freqs
        slot = lax.rem(batch, SLOTS)
        return pltpu.make_async_copy(
            kernel_ref.at[:, freq, pl.ds(row_tile * TILE, TILE), pl.ds(column * TILE, TILE)],
            slots.at[slot, which],
            slot_sems.at[slot, which],
        )

    def start(batch):
        @pl.when(batch < batches)
        def _():
            for which in range(BATCH):
                tile_copy(batch, which).start()

    mine = place_ref[parts]
    groups = len(field_refs) // parts
    copies = []
    for index, field_ref in enumerate(field_refs):
        part, group = index // groups, index % groups
        size = field_ref.shape[0]
        target = fields.at[place_ref[part], pl.ds(group * size, size)]
        copies.append(pltpu.make_async_copy(field_ref, target, field_sems.at[index]))
    for copy in copies:
        copy.start()
    for batch in range(SLOTS - 1):
        start(batch)

    def clear(line, _):
        sums[line] = jnp.zeros((TILE, lanes), F32)
        return 0

    lax.fori_loop(0, lines, clear, 0)
    for copy in copies:
        copy.wait()

    left = lax.broadcasted_iota(jnp.int32, (TILE, lanes), 1) < half

    def batch_step(batch, _):
        start(batch + SLOTS - 1)
        slot = lax.rem(batch, SLOTS)
        results = []
        for which in range(BATCH):
            tile_copy(batch, which).wait()
        for which in range(BATCH):
            code = tiles_ref[batch * BATCH + which]
            column, line = lax.rem(code, column_tiles), code // column_tiles
            part, first = column // tiles_per_part, lax.rem(column, tiles_per_part) * per_tile
            freq = lax.rem(line, freqs)
            field = [fields[part, lax.bitwise_xor(first + k, mine), freq] for k in range(per_tile)]
            field = jnp.concatenate(field, axis=0)
            swapped = pltpu.roll(field.astype(F32), half, 1)
            swapped = jnp.where(left, -swapped, swapped).astype(BF16)
            both = jnp.concatenate([slots[slot, which, 0], slots[slot, which, 1]], axis=1)
            results.append((line, dot(both, jnp.concatenate([field, swapped], axis=0))))
        for line, result in results:
            sums[line] += result
        return 0

    lax.fori_loop(0, batches, batch_step, 0)

    def finish(line, _):
        freq, row_tile = lax.rem(line, freqs), line // freqs
        bands = sums[line].astype(BF16).reshape(per_tile, depth, lanes)
        out_ref[pl.ds(row_tile * per_tile, per_tile), freq] = bands
        return 0

    lax.fori_loop(0, lines, finish, 0)


def product_call(tiles, count, places, kernel, fields, parts):
    owners = sum(field.shape[0] for field in fields) // parts
    _, freqs, depth, lanes = fields[0].shape
    lines = kernel.shape[2] // TILE * freqs
    smem = pl.BlockSpec(memory_space=pltpu.SMEM)
    anywhere = pl.BlockSpec(memory_space=pl.ANY)
    return pl.pallas_call(
        functools.partial(product_kernel, parts=parts),
        in_specs=[smem, smem, smem, anywhere] + [anywhere] * len(fields),
        out_specs=pl.BlockSpec(memory_space=pltpu.VMEM),
        out_shape=jax.ShapeDtypeStruct((owners, freqs, depth, lanes), BF16),
        scratch_shapes=[
            pltpu.VMEM((parts, owners, freqs, depth, lanes), BF16),
            pltpu.VMEM((lines + 1, TILE, lanes), F32),
            pltpu.VMEM((SLOTS, BATCH, 2, TILE, TILE), BF16),
            pltpu.SemaphoreType.DMA((SLOTS, BATCH)),
            pltpu.SemaphoreType.DMA((len(fields),)),
        ],
        compiler_params=pltpu.CompilerParams(vmem_limit_bytes=VMEM_LIMIT),
        cost_estimate=pl.CostEstimate(
            flops=2 * kernel.size * lanes // 8, bytes_accessed=kernel.size // 4, transcendentals=0
        ),
    )(tiles, count, places, kernel, *fields)


def collect_kernel(*refs):
    blocks, (out_ref, sems) = refs[:-2], refs[-2:]
    copies = [
        pltpu.make_async_copy(block, out_ref.at[place], sems.at[place]) for place, block in enumerate(blocks)
    ]
    for copy in copies:
        copy.start()
    for copy in copies:
        copy.wait()


def collect_call(blocks):
    size = len(blocks) * blocks[0].size
    return pl.pallas_call(
        collect_kernel,
        in_specs=[pl.BlockSpec(memory_space=pl.ANY)] * len(blocks),
        out_specs=pl.BlockSpec(memory_space=pltpu.VMEM),
        out_shape=jax.ShapeDtypeStruct((len(blocks),) + blocks[0].shape, BF16),
        scratch_shapes=[pltpu.SemaphoreType.DMA((len(blocks),))],
        compiler_params=pltpu.CompilerParams(vmem_limit_bytes=VMEM_LIMIT),
        cost_estimate=pl.CostEstimate(flops=0, bytes_accessed=4 * size, transcendentals=0),
    )(*blocks)


def local(kernel, tile_mask, direct, onsets, *, owners, halves):
    receivers, focal, _ = direct.shape
    tables = phase_tables()
    onsets = onsets.reshape(receivers // GROUP, GROUP, focal).transpose(0, 2, 1)
    row, mine = lax.axis_index("rows"), lax.axis_index("freq").astype(jnp.int32)
    places = [lax.rem(row - shift + halves, halves) for shift in range(halves)]
    places = jnp.stack([*places, mine]).astype(jnp.int32)
    mine = mine[None]
    tiles, count = list_call(tile_mask)

    def time_at(kind, chunk, *operands):
        return time_call(kind, chunk, owners, mine, direct, tables, *operands)

    def spread(blocks):
        got = list(blocks)
        for shift in range(1, owners):
            pairs = [(place, place ^ shift) for place in range(owners)]
            got[shift] = lax.ppermute(blocks[shift], "freq", pairs)
        size = owners // REACHES
        fields = [[] for _ in range(halves)]
        for reach in range(REACHES):
            mine = collect_call(got[reach * size : (reach + 1) * size])
            fields[0].append(mine)
            for shift in range(1, halves):
                ring = [(place, (place + shift) % halves) for place in range(halves)]
                fields[shift].append(lax.ppermute(mine, "rows", ring))
        return [field for of_shift in fields for field in of_shift]

    def gather(bands):
        return lax.all_to_all(bands, "freq", 0, 0, tiled=True)

    blocks = [time_at("first", chunk) for chunk in range(CHUNKS)]
    out = None
    for turn in range(ITERS):
        bands = [None] * CHUNKS
        for chunk in range(CHUNKS):
            fields = spread(blocks[chunk])
            bands[chunk] = product_call(tiles, count, places, kernel, fields, halves)
        bands = [gather(bands[chunk]) for chunk in range(CHUNKS)]
        for chunk in range(CHUNKS):
            if turn + 1 < ITERS:
                blocks[chunk] = time_at("middle", chunk, onsets, bands[chunk])
            else:
                out = time_at("last", chunk, onsets, bands[chunk], out)
    return out


def solution(mesh):
    owners, halves = mesh.shape["freq"], mesh.shape["rows"]
    return jax.shard_map(
        functools.partial(local, owners=owners, halves=halves),
        mesh=mesh,
        in_specs=(
            P(None, "freq", "rows", None),
            P("freq", "rows", None),
            P(("rows", "freq"), None, None),
            P(("rows", "freq"), None),
        ),
        out_specs=P(("rows", "freq"), None, None),
        check_vma=False,
    )
```

```python
import functools
import math

import jax
import jax.numpy as jnp
from jax import lax
from jax.experimental import pallas as pl
from jax.experimental.pallas import tpu as pltpu
from jax.sharding import PartitionSpec as P


NF = 128
NT = 512
TILE = 128
ITERS = 2
LANES = 128
CHUNKS = 2
GROUP = 16
QUAD = 4
SLOTS = 3
BATCH = 16
REACHES = 2
MERGED = (0,)
F32 = jnp.float32
BF16 = jnp.bfloat16
VMEM_LIMIT = 24 * 1024 * 1024
TIME_VMEM_LIMIT = 50 * 1024 * 1024


def phase_tables():
    freq_ids = jnp.arange(NF, dtype=jnp.int32) + 1
    time_ids = jnp.arange(NT // 2, dtype=jnp.int32)
    phase_ids = freq_ids[:, None] * time_ids[None, :] % NT
    angles = phase_ids.astype(F32) * (2.0 * math.pi / NT)
    norm_scale = math.sqrt(2.0 / NT)
    table = jnp.stack([jnp.cos(angles), -jnp.sin(angles)]) * norm_scale
    table = table.reshape(2, NF // 2, 2, NT // 2).transpose(2, 0, 1, 3).reshape(2, NF, NT // 2)
    high = lax.reduce_precision(table, 8, 7)
    return jnp.concatenate([high, table - high], axis=1).astype(BF16)


def dot(a, b, dims=(1, 0)):
    return lax.dot_general(
        a, b, (((dims[0],), (dims[1],)), ((), ())), preferred_element_type=F32
    )


def split(x):
    high = x.astype(BF16)
    return high, (x - high.astype(F32)).astype(BF16)


def parity_rows(parity, receiver):
    return pl.ds(parity * GROUP + receiver, NF // 2, stride=2 * GROUP)


def to_rows(series, tables_ref, rows_ref, half, first):
    early, late = series[:, : NT // 2], series[:, NT // 2 :]
    for parity, folded in ((0, early - late), (1, early + late)):
        high, low = split(folded)
        both = dot(tables_ref[parity], high, (1, 1))
        spectra = both[:NF] + both[NF:] + dot(tables_ref[parity, :NF], low, (1, 1))
        for place in range(QUAD * half // LANES):
            pair = spectra[:, place * LANES : (place + 1) * LANES]
            real, imag = pair[: NF // 2], pair[NF // 2 :]
            left = lax.broadcasted_iota(jnp.int32, real.shape, 1) < half
            rows_ref[parity_rows(parity, first + 2 * place), :] = jnp.where(
                left, real, pltpu.roll(imag, half, 1)
            )
            rows_ref[parity_rows(parity, first + 2 * place + 1), :] = jnp.where(
                left, pltpu.roll(real, half, 1), imag
            )


def to_traces(rows_ref, tables_ref, half, first):
    odd, even = [], []
    for receiver in range(first, first + QUAD):
        rows = [rows_ref[parity_rows(parity, receiver), :] for parity in range(2)]
        turned = jnp.concatenate(rows, axis=0).T
        real, imag = turned[:half], turned[half:]
        left = lax.broadcasted_iota(jnp.int32, real.shape, 1) < NF // 2
        odd.append(jnp.where(left, real, pltpu.roll(imag, NF // 2, 1)))
        even.append(jnp.where(left, pltpu.roll(real, NF // 2, 1), imag))
    parts = []
    for parity, spectra in enumerate((odd, even)):
        spectra = jnp.concatenate(spectra, axis=0).astype(BF16)
        parts.append(dot(jnp.concatenate([spectra, spectra], axis=1), tables_ref[parity]))
    odd, even = parts
    return jnp.concatenate([even + odd, even - odd], axis=1)


def subtracted(direct_ref, traces, onsets_ref, half, first):
    series = direct_ref[first : first + QUAD].reshape(QUAD * half, NT)
    columns = [onsets_ref[0, :, first + which : first + which + 1] for which in range(QUAD)]
    ends = jnp.concatenate(columns, axis=0)
    times = lax.broadcasted_iota(jnp.int32, traces.shape, 1)
    return series - jnp.where(times < ends, traces, 0.0)


def store_out(out_refs, rows_ref, mine):
    for shift, out_ref in enumerate(out_refs):
        owner = lax.bitwise_xor(mine, shift)
        size = NF // len(out_refs) * GROUP
        rows = rows_ref[pl.ds(pl.multiple_of(owner * size, size), size), :]
        out_ref[...] = rows.reshape(out_ref.shape).astype(BF16)


def load_in(rows_ref, bands_refs, mine):
    if len(bands_refs) == 1:
        rows_ref[...] = bands_refs[0][...].astype(F32).reshape(NF * GROUP, LANES)
        return
    size = NF // len(bands_refs) * GROUP
    for shift, bands_ref in enumerate(bands_refs):
        owner = lax.bitwise_xor(mine, shift)
        rows = bands_ref[...].astype(F32).reshape(size, LANES)
        rows_ref[pl.ds(pl.multiple_of(owner * size, size), size), :] = rows


def first_kernel(mine_ref, direct_ref, tables_ref, *rest, half, sources):
    out_refs, rows_ref = rest[:-1], rest[-1]
    for first in range(0, GROUP, QUAD):
        series = direct_ref[first : first + QUAD].reshape(QUAD * half, NT)
        to_rows(series, tables_ref, rows_ref, half, first)
    store_out(out_refs, rows_ref, mine_ref[0])


def middle_kernel(mine_ref, direct_ref, tables_ref, onsets_ref, *rest, half, sources):
    bands_refs, out_refs, (in_rows, rows_ref) = rest[:sources], rest[sources:-2], rest[-2:]
    load_in(in_rows, bands_refs, mine_ref[0])
    for first in range(0, GROUP, QUAD):
        traces = to_traces(in_rows, tables_ref, half, first)
        series = subtracted(direct_ref, traces, onsets_ref, half, first)
        to_rows(series, tables_ref, rows_ref, half, first)
    store_out(out_refs, rows_ref, mine_ref[0])


def last_kernel(mine_ref, direct_ref, tables_ref, onsets_ref, *rest, half, sources):
    bands_refs, (out_ref, in_rows) = rest[:sources], rest[-2:]
    load_in(in_rows, bands_refs, mine_ref[0])
    for first in range(0, GROUP, QUAD):
        traces = to_traces(in_rows, tables_ref, half, first)
        series = subtracted(direct_ref, traces, onsets_ref, half, first)
        out_ref[first : first + QUAD] = series.reshape(QUAD, half, NT)


def time_call(kind, chunk, owners, mine, direct, tables, onsets=None, bands=None, out=None):
    receivers, focal, _ = direct.shape
    half = focal // CHUNKS
    freqs = NF // owners
    series_spec = pl.BlockSpec((GROUP, half, NT), lambda g: (g, chunk, 0))
    rows_spec = pl.BlockSpec((owners, freqs, GROUP, LANES), lambda g: (0, 0, g, 0))
    operands = [mine, direct, tables]
    specs = [pl.BlockSpec(memory_space=pltpu.SMEM), series_spec, pl.BlockSpec((2, 2 * NF, NT // 2), lambda g: (0, 0, 0))]
    block_spec = pl.BlockSpec((freqs, GROUP, LANES), lambda g: (0, g, 0))
    bands = bands or []
    if kind != "first":
        operands += [onsets, *bands]
        specs.append(pl.BlockSpec((1, half, GROUP), lambda g: (g, chunk, 0)))
        specs += [rows_spec] if len(bands) == 1 else [block_spec] * owners
    aliases = {}
    if out is not None:
        aliases = {len(operands): 0}
        operands.append(out)
        specs.append(pl.BlockSpec(memory_space=pl.ANY))
    rows_scratch = pltpu.VMEM((NF * GROUP, LANES), F32)
    if kind == "last":
        out_specs, out_shape = series_spec, jax.ShapeDtypeStruct(direct.shape, F32)
    else:
        out_specs = [block_spec] * owners
        out_shape = [jax.ShapeDtypeStruct((freqs, receivers, LANES), BF16)] * owners
    body, passes, scratches = {
        "first": (first_kernel, 3, 1),
        "middle": (middle_kernel, 5, 2),
        "last": (last_kernel, 2, 1),
    }[kind]
    elements = receivers * half * NT
    return pl.pallas_call(
        functools.partial(body, half=half, sources=len(bands)),
        grid=(receivers // GROUP,),
        in_specs=specs,
        out_specs=out_specs,
        out_shape=out_shape,
        scratch_shapes=[rows_scratch] * scratches,
        input_output_aliases=aliases,
        compiler_params=pltpu.CompilerParams(vmem_limit_bytes=TIME_VMEM_LIMIT),
        cost_estimate=pl.CostEstimate(
            flops=4 * passes * elements * NF, bytes_accessed=8 * elements, transcendentals=0
        ),
    )(*operands)


def list_kernel(mask_ref, tiles_ref, count_ref):
    freqs, row_tiles, column_tiles = mask_ref.shape
    lines = row_tiles * freqs

    def row(line, position):
        row_tile, freq = line // freqs, lax.rem(line, freqs)
        for column in range(column_tiles):
            tiles_ref[position] = line * column_tiles + column
            position = position + jnp.where(mask_ref[freq, row_tile, column] != 0, 1, 0)
        return position

    total = lax.fori_loop(0, lines, row, 0)
    for extra in range(BATCH):
        tiles_ref[total + extra] = lines * column_tiles
    count_ref[0] = (total + BATCH - 1) // BATCH


def list_call(tile_mask):
    freqs, row_tiles, column_tiles = tile_mask.shape
    smem = pl.BlockSpec(memory_space=pltpu.SMEM)
    return pl.pallas_call(
        list_kernel,
        in_specs=[smem],
        out_specs=[smem, smem],
        out_shape=[
            jax.ShapeDtypeStruct((freqs * row_tiles * column_tiles + BATCH,), jnp.int32),
            jax.ShapeDtypeStruct((1,), jnp.int32),
        ],
        compiler_params=pltpu.CompilerParams(vmem_limit_bytes=1024 * 1024),
        name="list_tiles",
    )(tile_mask)


def product_kernel(tiles_ref, count_ref, place_ref, kernel_ref, *rest, parts, sources):
    field_refs, out_refs, scratch = rest[:sources], rest[sources:-6], rest[-6:]
    bands_ref, fields, sums, slots, slot_sems, field_sems = scratch
    out_ref = out_refs[0] if len(out_refs) == 1 else bands_ref
    _, _, rows, columns = kernel_ref.shape
    _, _, freqs, depth, lanes = fields.shape
    row_tiles, column_tiles = rows // TILE, columns // TILE
    lines = row_tiles * freqs
    per_tile = TILE // depth
    tiles_per_part = column_tiles // parts
    half = lanes // 2
    batches = count_ref[0]

    def tile_copy(batch, which):
        code = tiles_ref[batch * BATCH + which]
        column = lax.rem(code, column_tiles)
        line = jnp.minimum(code // column_tiles, lines - 1)
        freq, row_tile = lax.rem(line, freqs), line // freqs
        slot = lax.rem(batch, SLOTS)
        return pltpu.make_async_copy(
            kernel_ref.at[:, freq, pl.ds(row_tile * TILE, TILE), pl.ds(column * TILE, TILE)],
            slots.at[slot, which],
            slot_sems.at[slot, which],
        )

    def start(batch):
        @pl.when(batch < batches)
        def _():
            for which in range(BATCH):
                tile_copy(batch, which).start()

    mine = place_ref[parts]
    groups = len(field_refs) // parts
    copies = []
    for index, field_ref in enumerate(field_refs):
        part, group = index // groups, index % groups
        size = field_ref.shape[0]
        target = fields.at[place_ref[part], pl.ds(group * size, size)]
        copies.append(pltpu.make_async_copy(field_ref, target, field_sems.at[index]))
    for copy in copies:
        copy.start()
    for batch in range(SLOTS - 1):
        start(batch)

    def clear(line, _):
        sums[line] = jnp.zeros((TILE, lanes), F32)
        return 0

    lax.fori_loop(0, lines, clear, 0)
    for copy in copies:
        copy.wait()

    left = lax.broadcasted_iota(jnp.int32, (TILE, lanes), 1) < half

    def batch_step(batch, _):
        start(batch + SLOTS - 1)
        slot = lax.rem(batch, SLOTS)
        results = []
        for which in range(BATCH):
            tile_copy(batch, which).wait()
        for which in range(BATCH):
            code = tiles_ref[batch * BATCH + which]
            column, line = lax.rem(code, column_tiles), code // column_tiles
            part, first = column // tiles_per_part, lax.rem(column, tiles_per_part) * per_tile
            freq = lax.rem(line, freqs)
            field = [fields[part, lax.bitwise_xor(first + k, mine), freq] for k in range(per_tile)]
            field = jnp.concatenate(field, axis=0)
            swapped = pltpu.roll(field.astype(F32), half, 1)
            swapped = jnp.where(left, -swapped, swapped).astype(BF16)
            both = jnp.concatenate([slots[slot, which, 0], slots[slot, which, 1]], axis=1)
            results.append((line, dot(both, jnp.concatenate([field, swapped], axis=0))))
        for line, result in results:
            sums[line] += result
        return 0

    lax.fori_loop(0, batches, batch_step, 0)

    def finish(line, _):
        freq, row_tile = lax.rem(line, freqs), line // freqs
        bands = sums[line].astype(BF16).reshape(per_tile, depth, lanes)
        out_ref[pl.ds(row_tile * per_tile, per_tile), freq] = bands
        return 0

    lax.fori_loop(0, lines, finish, 0)
    if len(out_refs) > 1:
        for shift, block_ref in enumerate(out_refs):
            block_ref[...] = bands_ref[lax.bitwise_xor(mine, shift)]


def product_call(chunk, tiles, count, places, kernel, fields, parts):
    owners = sum(field.shape[0] for field in fields) // parts
    _, freqs, depth, lanes = fields[0].shape
    lines = kernel.shape[2] // TILE * freqs
    smem = pl.BlockSpec(memory_space=pltpu.SMEM)
    anywhere = pl.BlockSpec(memory_space=pl.ANY)
    return pl.pallas_call(
        functools.partial(product_kernel, parts=parts, sources=len(fields)),
        in_specs=[smem, smem, smem, anywhere] + [anywhere] * len(fields),
        out_specs=[pl.BlockSpec(memory_space=pltpu.VMEM)] * (1 if chunk in MERGED else owners),
        out_shape=[jax.ShapeDtypeStruct((owners, freqs, depth, lanes), BF16)]
        if chunk in MERGED
        else [jax.ShapeDtypeStruct((freqs, depth, lanes), BF16)] * owners,
        scratch_shapes=[
            pltpu.VMEM((8, 128) if chunk in MERGED else (owners, freqs, depth, lanes), BF16),
            pltpu.VMEM((parts, owners, freqs, depth, lanes), BF16),
            pltpu.VMEM((lines + 1, TILE, lanes), F32),
            pltpu.VMEM((SLOTS, BATCH, 2, TILE, TILE), BF16),
            pltpu.SemaphoreType.DMA((SLOTS, BATCH)),
            pltpu.SemaphoreType.DMA((len(fields),)),
        ],
        compiler_params=pltpu.CompilerParams(vmem_limit_bytes=VMEM_LIMIT),
        cost_estimate=pl.CostEstimate(
            flops=2 * kernel.size * lanes // 8, bytes_accessed=kernel.size // 4, transcendentals=0
        ),
    )(tiles, count, places, kernel, *fields)


def collect_kernel(*refs):
    blocks, (out_ref, sems) = refs[:-2], refs[-2:]
    copies = [
        pltpu.make_async_copy(block, out_ref.at[place], sems.at[place]) for place, block in enumerate(blocks)
    ]
    for copy in copies:
        copy.start()
    for copy in copies:
        copy.wait()


def collect_call(blocks):
    size = len(blocks) * blocks[0].size
    return pl.pallas_call(
        collect_kernel,
        in_specs=[pl.BlockSpec(memory_space=pl.ANY)] * len(blocks),
        out_specs=pl.BlockSpec(memory_space=pltpu.VMEM),
        out_shape=jax.ShapeDtypeStruct((len(blocks),) + blocks[0].shape, BF16),
        scratch_shapes=[pltpu.SemaphoreType.DMA((len(blocks),))],
        compiler_params=pltpu.CompilerParams(vmem_limit_bytes=VMEM_LIMIT),
        cost_estimate=pl.CostEstimate(flops=0, bytes_accessed=4 * size, transcendentals=0),
    )(*blocks)


def local(kernel, tile_mask, direct, onsets, *, owners, halves):
    receivers, focal, _ = direct.shape
    tables = phase_tables()
    onsets = onsets.reshape(receivers // GROUP, GROUP, focal).transpose(0, 2, 1)
    row, mine = lax.axis_index("rows"), lax.axis_index("freq").astype(jnp.int32)
    places = [lax.rem(row - shift + halves, halves) for shift in range(halves)]
    places = jnp.stack([*places, mine]).astype(jnp.int32)
    mine = mine[None]
    tiles, count = list_call(tile_mask)

    def time_at(kind, chunk, *operands):
        return time_call(kind, chunk, owners, mine, direct, tables, *operands)

    def permuted(blocks):
        got = list(blocks)
        for shift in range(1, owners):
            pairs = [(place, place ^ shift) for place in range(owners)]
            got[shift] = lax.ppermute(blocks[shift], "freq", pairs)
        return got

    def spread(blocks):
        got = permuted(blocks)
        size = owners // REACHES
        fields = [[] for _ in range(halves)]
        for reach in range(REACHES):
            mine = collect_call(got[reach * size : (reach + 1) * size])
            fields[0].append(mine)
            for shift in range(1, halves):
                ring = [(place, (place + shift) % halves) for place in range(halves)]
                fields[shift].append(lax.ppermute(mine, "rows", ring))
        return [field for of_shift in fields for field in of_shift]

    def gather(bands, chunk):
        if chunk in MERGED:
            return [lax.all_to_all(bands[0], "freq", 0, 0, tiled=True)]
        return permuted(bands)

    blocks = [time_at("first", chunk) for chunk in range(CHUNKS)]
    out = None
    for turn in range(ITERS):
        bands = [None] * CHUNKS
        for chunk in range(CHUNKS):
            fields = spread(blocks[chunk])
            bands[chunk] = product_call(chunk, tiles, count, places, kernel, fields, halves)
        bands = [gather(bands[chunk], chunk) for chunk in range(CHUNKS)]
        for chunk in range(CHUNKS):
            if turn + 1 < ITERS:
                blocks[chunk] = time_at("middle", chunk, onsets, bands[chunk])
            else:
                out = time_at("last", chunk, onsets, bands[chunk], out)
    return out


def solution(mesh):
    owners, halves = mesh.shape["freq"], mesh.shape["rows"]
    return jax.shard_map(
        functools.partial(local, owners=owners, halves=halves),
        mesh=mesh,
        in_specs=(
            P(None, "freq", "rows", None),
            P("freq", "rows", None),
            P(("rows", "freq"), None, None),
            P(("rows", "freq"), None),
        ),
        out_specs=P(("rows", "freq"), None, None),
        check_vma=False,
    )
```
